256 devices in a mesh: dim: 8 (over y, core), rows: 32 (over x, z).
Axes of the slice: x: 4, y: 4, z: 8, core: 2. Of those that a mesh axis runs over, the one named last changes fastest.
Arguments:
- user_rows: bfloat16 [2048, 2048], P('rows', 'dim'), may hold values from -0.125 to 0.125
- item_table: bfloat16 [32768, 2048], P('rows', 'dim')
- observed_items: int32 [2048, 32], P('rows'), may hold values from 0 to 32767, as said below
- counts: int32 [2048], P('rows'), may hold values from 1 to 32
- item_row: int32 [32768], replicated, may hold values from 0 to 32767, as said below
Outputs:
- new_users: float32 [2048, 2048], P('rows', 'dim')
The draws below stay inside these ranges and needn't reach their ends.
Inputs may be any that keep to these rules, and one draw needn't show every extreme that they name: item_row is a permutation; rows k * 1024 to (k + 1) * 1024 - 1 of item_table form item block k. In the rows of observed_items of each 64 consecutive users (padding slots included), exactly 64 slots name items whose table row lies in item block k, for every k.
All inputs are finite; a program needn't handle non-finite values.
Results may differ from the reference program's by a relative error of at most 0.0003.
Values may be sent and summed in bfloat16 or wider, within the bound.
No kernel may reach another device: no remote copies, remote signals or barrier semaphores. Data moves between devices by JAX's collectives and lax.ppermute only.
A program may use at most 64 MiB of HBM per device.

```python
import jax
import jax.numpy as jnp
from jax import lax

BLOCK = 256
LIST = 32
USERS_DEV = 64
ITEM_DEV = 1024
EMBED = 2048
ITEMS = 32768
USERS = 2048
N_ROWS = 32


def cluster_count():
    return max(ITEM_DEV // 16, 1)


def shared_layout(key):
    folded = jax.random.fold_in(key, 11)
    perm_key, owner_key, slot_key, taste_key = jax.random.split(folded, 4)
    item_order = jax.random.permutation(perm_key, ITEMS).astype(jnp.int32)
    slots_dev = USERS_DEV * LIST
    per_owner = slots_dev // N_ROWS
    nclusters = cluster_count()
    members = ITEM_DEV // nclusters

    def one_device(device_index):
        owners = jax.random.permutation(jax.random.fold_in(owner_key, device_index), slots_dev).astype(jnp.int32) // per_owner
        tastes = jax.random.randint(jax.random.fold_in(taste_key, device_index), (USERS_DEV, 2), 0, nclusters, dtype=jnp.int32)
        slot_index = jnp.arange(slots_dev, dtype=jnp.int32)
        user_local = slot_index // LIST
        position = slot_index % LIST
        chosen = jnp.where(position % 2 == 0, tastes[user_local, 0], tastes[user_local, 1])
        member = jax.random.randint(jax.random.fold_in(slot_key, device_index), (slots_dev,), 0, members, dtype=jnp.int32)
        within = chosen + nclusters * member
        return owners * ITEM_DEV + within
    table_slots = jax.vmap(one_device)(jnp.arange(N_ROWS, dtype=jnp.int32))
    inverse_order = jnp.argsort(item_order).astype(jnp.int32)
    item_ids = inverse_order[table_slots.reshape(-1)].reshape(USERS, LIST)
    return (item_order, item_ids)


def draw_item_row(key, part):
    return shared_layout(key)[0]


def draw_observed_items(key, part):
    return shared_layout(key)[1]


def draw_item_table(key, part):
    folded = jax.random.fold_in(key, 3)
    noise_key, scale_key, center_key, load_key = jax.random.split(folded, 4)
    nclusters = cluster_count()
    factors = 16
    noise_part = jax.random.normal(noise_key, (ITEMS, EMBED), jnp.float32)
    centers = jax.random.normal(center_key, (factors, nclusters, EMBED), jnp.float32)
    loadings = jax.random.normal(load_key, (ITEMS, factors), jnp.float32)
    item_scale = jnp.exp(jax.random.uniform(scale_key, (ITEMS, 1), jnp.float32, -1.0, 1.0))
    row_cluster = jnp.arange(ITEMS, dtype=jnp.int32) % ITEM_DEV % nclusters
    signal = jnp.zeros((ITEMS, EMBED), jnp.float32)
    for factor_index in range(factors):
        weight_now = 0.6 * 10.0 ** (-1.5 * factor_index / (factors - 1))
        signal = signal + (weight_now * loadings[:, factor_index])[:, None] * centers[factor_index][row_cluster]
    return (item_scale * (signal + 0.3 * noise_part)).astype(jnp.bfloat16)


def touch_ends(drawn, key, smallest, largest):
    spot = [jax.random.randint(jax.random.fold_in(key, axis), (), 0, length) for axis, length in enumerate(drawn.shape)]
    longest = drawn.shape.index(max(drawn.shape))
    next_to = spot[:longest] + [(spot[longest] + 1) % drawn.shape[longest]] + spot[longest + 1:]
    return drawn.at[tuple(spot)].set(smallest).at[tuple(next_to)].set(largest)


def levels(key, shape, shards, smallest, top_value):
    gain = 1.0
    for dim, blocks in shards:
        heights = jax.random.uniform(jax.random.fold_in(jax.random.fold_in(key, 6), dim), (blocks,), jnp.float32, smallest / len(shards), top_value / len(shards))
        gain = gain * jnp.repeat(jnp.exp(heights), shape[dim] // blocks).reshape((-1,) + (1,) * (len(shape) - 1 - dim))
    return gain


def centred(rng, shape, deviation, reach, pieces=(), held_as=jnp.bfloat16):
    drawn = jax.random.normal(rng, shape, jnp.float32) * deviation
    if len(pieces) > 0:
        drawn = levels(rng, shape, pieces, -0.22, 0.18) * drawn
    return jnp.clip(drawn, min=-reach, max=reach).astype(held_as)


def setup_inputs(seed: int = 0) -> dict:
    seeds = jax.random.split(jax.random.key(seed), 6)
    return {
        "user_rows": centred(seeds[0], (USERS, EMBED), EMBED ** -0.5, 0.125, ((0, 32), (1, 8))),
        "item_table": draw_item_table(jax.random.fold_in(seeds[5], 71), 0),
        "observed_items": draw_observed_items(jax.random.fold_in(seeds[5], 71), 0),
        "counts": touch_ends(jax.random.randint(seeds[3], (USERS,), 1, LIST + 1), jax.random.fold_in(seeds[3], 1), 1, LIST).astype(jnp.int32),
        "item_row": draw_item_row(jax.random.fold_in(seeds[5], 71), 0),
    }


def reference(user_rows, item_table, observed_items, counts, item_row):
    highest = lax.Precision.HIGHEST
    nblocks = EMBED // BLOCK
    weight_unobs = 32.0 / ITEMS
    gram_matrix = jnp.dot(item_table.T.astype(jnp.float32), item_table.astype(jnp.float32), preferred_element_type=jnp.float32)
    gram_times = jnp.dot(user_rows.astype(jnp.float32), gram_matrix, precision=highest)
    diag_blocks = jnp.stack([gram_matrix[n * BLOCK:(n + 1) * BLOCK, n * BLOCK:(n + 1) * BLOCK] for n in range(nblocks)])
    diag_shift = weight_unobs * diag_blocks + jnp.eye(BLOCK, dtype=jnp.float32)
    table_rows = item_row[observed_items]
    live = (lax.broadcasted_iota(jnp.int32, (USERS, LIST), 1) < counts[:, None]).astype(jnp.float32)

    def solve_users(inputs):
        users_here, rows_here, live_here, times_here = inputs
        fetched = item_table[rows_here].astype(jnp.float32)
        predicted = jnp.einsum('ue,uje->uj', users_here.astype(jnp.float32), fetched, precision=highest)
        residual = live_here * (predicted - 1.0)
        fetched_blocks = fetched.reshape(8, LIST, nblocks, BLOCK) * live_here[:, :, None, None]
        hessian = jnp.einsum('ujna,ujnb->unab', fetched_blocks, fetched_blocks, precision=highest) + diag_shift
        own_blocks = users_here.astype(jnp.float32).reshape(8, nblocks, BLOCK)
        gradient = jnp.einsum('uj,ujnb->unb', residual, fetched_blocks, precision=highest)
        gradient = gradient + weight_unobs * times_here.reshape(8, nblocks, BLOCK) + own_blocks
        factor = jnp.linalg.cholesky(hessian)
        middle = jax.scipy.linalg.solve_triangular(factor, gradient[..., None], lower=True)
        update = jax.scipy.linalg.solve_triangular(factor, middle, lower=True, trans='T')[..., 0]
        return (own_blocks - update).reshape(8, EMBED)
    result = lax.map(solve_users, (user_rows.reshape(-1, 8, EMBED), table_rows.reshape(-1, 8, LIST), live.reshape(-1, 8, LIST), gram_times.reshape(-1, 8, EMBED)))
    return result.reshape(USERS, EMBED)
```

```python
import jax
import jax.numpy as jnp
from jax import lax
from jax.experimental import pallas as pl
from jax.experimental.pallas import tpu as pltpu
from jax.sharding import Mesh, PartitionSpec as P

F32 = jnp.float32
BF16 = jnp.bfloat16
I32 = jnp.int32
ROWS = ("x", "z")
DIM = ("y", "core")
BLOCK = 256
LIST = 32
USERS_DEV = 64
SLOTS = USERS_DEV * LIST
ITEM_DEV = 1024
N_ROWS = 32
N_DIM = 8
PER = SLOTS // N_ROWS
CHUNK = 256
CHUNKS = SLOTS // CHUNK
WEIGHT = 32.0 / 32768.0
VMEM = pl.BlockSpec(memory_space=pltpu.VMEM)
SMEM = pl.BlockSpec(memory_space=pltpu.SMEM)


def iota(shape, dim):
    return lax.broadcasted_iota(I32, shape, dim)


def dot(a, b, ca=1, cb=0):
    return lax.dot_general(a, b, (((ca,), (cb,)), ((), ())), preferred_element_type=F32)


def split(a):
    top = a.astype(BF16)
    rest = a - top.astype(F32)
    mid = rest.astype(BF16)
    low = (rest - mid.astype(F32)).astype(BF16)
    return top, mid, low


def dot_split(a, b):
    a0, a1, a2 = a
    b0, b1, b2 = b
    small = dot(a2, b0) + dot(a0, b2) + dot(a1, b1)
    return (small + (dot(a1, b0) + dot(a0, b1))) + dot(a0, b0)


def one_hot(column, width):
    hit = iota((column.shape[0], width), 1) == column
    return jnp.where(hit, 1.0, 0.0).astype(BF16)


def call(kernel, out_shape, n_in, flops, nbytes, scratch=(), in_specs=None):
    multi = isinstance(out_shape, (tuple, list))
    return pl.pallas_call(
        kernel,
        out_shape=out_shape,
        in_specs=in_specs or [VMEM] * n_in,
        out_specs=[VMEM] * len(out_shape) if multi else VMEM,
        scratch_shapes=list(scratch),
        compiler_params=pltpu.CompilerParams(vmem_limit_bytes=48 << 20),
        cost_estimate=pl.CostEstimate(flops=flops, bytes_accessed=nbytes, transcendentals=0),
    )


def index_kernel(ids_ref, table_ref, pos_ref, req_ref):
    table = table_ref[...]
    table_hi = (table >> 8).astype(F32).astype(BF16)
    table_lo = (table & 255).astype(F32).astype(BF16)
    lane = iota((CHUNK, 128), 1)
    before = jnp.where(
        iota((CHUNK, CHUNK), 0) > iota((CHUNK, CHUNK), 1), 1.0, 0.0
    ).astype(BF16)
    totals = jnp.zeros((1, 128), F32)
    asked = jnp.zeros((128, SLOTS), F32)
    for c in range(CHUNKS):
        ids = ids_ref[c * CHUNK : (c + 1) * CHUNK, :]
        picked = one_hot(ids >> 7, 256)
        values = dot(picked, table_hi) * 256.0 + dot(picked, table_lo)
        row = jnp.sum(jnp.where(lane == (ids & 127), values, 0.0), axis=1, keepdims=True)
        row = row.astype(I32)
        member = jnp.where(lane == (row >> 10), 1.0, 0.0)
        rank = dot(before, member.astype(BF16)) + totals
        place = rank + (lane * PER).astype(F32)
        pos = jnp.sum(member * place, axis=1, keepdims=True).astype(I32)
        totals = totals + jnp.sum(member, axis=0, keepdims=True)
        pos_ref[c * CHUNK : (c + 1) * CHUNK, :] = pos
        within = row & 1023
        parts = jnp.where(lane == 0, within >> 5, jnp.where(lane == 1, within & 31, 0))
        asked = asked + dot(parts.astype(F32).astype(BF16), one_hot(pos, SLOTS), 0, 0)
    req_ref[...] = (asked[0:1, :] * 32.0 + asked[1:2, :]).astype(I32)


def pick_kernel(req_ref, table_ref, rows_ref):
    table = table_ref[...]
    for c in range(CHUNKS):
        part = slice(c * CHUNK, (c + 1) * CHUNK)
        rows_ref[part, :] = dot(one_hot(req_ref[part, :], ITEM_DEV), table).astype(BF16)


def place_kernel(pos_ref, came_ref, users_ref, fetched_ref, pred_ref):
    came = came_ref[...]
    users = users_ref[...]
    lane = iota((LIST, USERS_DEV), 1)
    pred = jnp.zeros((LIST, USERS_DEV), F32)
    for c in range(CHUNKS):
        part = slice(c * CHUNK, (c + 1) * CHUNK)
        rows = dot(one_hot(pos_ref[part, :], SLOTS), came).astype(BF16)
        fetched_ref[part, :] = rows
        cross = dot(rows, users, 1, 1)
        for i in range(CHUNK // LIST):
            user = c * (CHUNK // LIST) + i
            pred = pred + jnp.where(lane == user, cross[i * LIST : (i + 1) * LIST, :], 0.0)
    pred_ref[...] = pred


def product_kernel(block_ref, users_ref, *refs):
    tables, out_ref = refs[:N_DIM], refs[N_DIM]
    scores = jnp.zeros((BLOCK, ITEM_DEV), F32)
    for i in range(N_DIM):
        scores = scores + dot(users_ref[block_ref[i]], tables[i][...], 1, 1)
    s0, s1, s2 = split(scores)
    for i in range(N_DIM):
        table = tables[i][...]
        times = (dot(s2, table) + dot(s1, table)) + dot(s0, table)
        first = pl.multiple_of(block_ref[i] * BLOCK, BLOCK)
        out_ref[:, pl.ds(first, BLOCK)] = times


def inverse_kernel(diag_ref, out_ref, work):
    eye = jnp.where(iota((BLOCK, BLOCK), 0) == iota((BLOCK, BLOCK), 1), 1.0, 0.0)
    work[...] = WEIGHT * diag_ref[...] + eye
    row_lane = iota((1, BLOCK), 1)
    half_lane = iota((128, 128), 1)
    for half in range(2):

        def step(k, carry):
            here = half * 128 + k
            row = work[pl.ds(here, 1), :]
            pivot = jnp.sum(jnp.where(row_lane == here, row, 0.0), axis=1, keepdims=True)
            inv = 1.0 / pivot
            scaled = row * inv
            for i in range(2):
                column = jnp.transpose(
                    jnp.broadcast_to(row[:, i * 128 : (i + 1) * 128], (128, 128))
                )
                for j in range(2):
                    at = (slice(i * 128, (i + 1) * 128), slice(j * 128, (j + 1) * 128))
                    new = work[at] - column * scaled[:, j * 128 : (j + 1) * 128]
                    if j == half:
                        new = jnp.where(half_lane == k, column * inv, new)
                    work[at] = new
            work[pl.ds(here, 1), :] = jnp.where(row_lane == here, -inv, scaled)
            return carry

        lax.fori_loop(0, 128, step, 0)
    out_ref[...] = -work[...]


def inner_kernel(fetched_ref, inverse_ref, counts_ref, out_ref, folded, work):
    i0, i1, i2 = split(inverse_ref[...])
    same = iota((CHUNK, CHUNK), 0) // LIST == iota((CHUNK, CHUNK), 1) // LIST
    for c in range(CHUNKS):
        part = slice(c * CHUNK, (c + 1) * CHUNK)
        rows = fetched_ref[part, :]
        scaled = (dot(rows, i2) + dot(rows, i1)) + dot(rows, i0)
        s0, s1, s2 = split(scaled)
        cross = (dot(s2, rows, 1, 1) + dot(s1, rows, 1, 1)) + dot(s0, rows, 1, 1)
        cross = jnp.where(same, cross, 0.0)
        both = cross[:, :128] + cross[:, 128:]
        both = both + pltpu.roll(both, 64, 1)
        folded[part, :] = both + pltpu.roll(both, 32, 1)
    slot = iota((LIST, USERS_DEV), 0)
    live = jnp.where(slot < counts_ref[...], 1.0, 0.0)
    for a in range(LIST):
        mine = jnp.transpose(folded[pl.ds(a, USERS_DEV, stride=LIST), :])[:LIST, :]
        work[a] = mine * (live * live[a : a + 1, :]) + jnp.where(slot == a, 1.0, 0.0)

    def step(k, carry):
        row = work[k]
        pivot = work[k, pl.ds(k, 1), :]
        inv = 1.0 / pivot
        scaled = row * inv
        here = slot == k
        for a in range(LIST):
            factor = row[a : a + 1, :]
            work[a] = jnp.where(here, factor * inv, work[a] - factor * scaled)
        work[k] = jnp.where(here, -inv, scaled)
        return carry

    lax.fori_loop(0, LIST, step, 0)
    out_ref[...] = -work[...]


def spread(values):
    flat = jnp.transpose(values)
    wide = jnp.concatenate([flat] * 4, axis=1)
    wide = jnp.concatenate([wide] * (SLOTS // 128), axis=1)
    own = iota((USERS_DEV, SLOTS), 1) // LIST == iota((USERS_DEV, SLOTS), 0)
    return jnp.where(own, wide, 0.0)


def weigh(values, fetched):
    s0, s1, s2 = split(spread(values))
    return (dot(s2, fetched) + dot(s1, fetched)) + dot(s0, fetched)


def final_kernel(
    fetched_ref, inverse_ref, inner_ref, counts_ref, pred_ref, users_ref, times_ref, out_ref
):
    fetched = fetched_ref[...]
    inverse = split(inverse_ref[...])
    own = users_ref[...].astype(F32)
    slot = iota((LIST, USERS_DEV), 0)
    lane = iota((LIST, USERS_DEV), 1)
    live = jnp.where(slot < counts_ref[...], 1.0, 0.0)
    pred = pred_ref[0]
    for i in range(1, N_DIM):
        pred = pred + pred_ref[i]
    residual = live * (pred - 1.0)
    gradient = weigh(residual, fetched) + WEIGHT * times_ref[...] + own
    scaled = dot_split(split(gradient), inverse)
    y0, y1, y2 = split(scaled)
    cross = (dot(fetched, y2, 1, 1) + dot(fetched, y1, 1, 1)) + dot(fetched, y0, 1, 1)
    projected = jnp.zeros((LIST, USERS_DEV), F32)
    for user in range(USERS_DEV):
        projected = projected + jnp.where(
            lane == user, cross[user * LIST : (user + 1) * LIST, :], 0.0
        )
    projected = projected * live
    weights = jnp.zeros((LIST, USERS_DEV), F32)
    for a in range(LIST):
        weights = weights + inner_ref[a] * projected[a : a + 1, :]
    weights = weights * live
    back = dot_split(split(weigh(weights, fetched)), inverse)
    out_ref[...] = own - (scaled - back)


def shape(dims, dtype):
    return jax.ShapeDtypeStruct(dims, dtype)


def gather_dims(table):
    up = [(i, (i + 1) % 4) for i in range(4)]
    down = [(i, (i + 3) % 4) for i in range(4)]
    swap = [(0, 1), (1, 0)]
    half = ITEM_DEV // 2
    next_y = lax.ppermute(table, "y", down)
    last_y = lax.ppermute(table, "y", up)
    far_top = lax.ppermute(next_y[:half], "y", down)
    far_low = lax.ppermute(last_y[half:], "y", up)
    far = jnp.concatenate([far_top, far_low], axis=0)
    tables = [table, next_y, far, last_y]
    others = [lax.ppermute(t, "core", swap) for t in tables]
    y = lax.axis_index("y")
    core = lax.axis_index("core")
    blocks = [((y + i) % 4) * 2 + core for i in range(4)]
    blocks += [((y + i) % 4) * 2 + (1 - core) for i in range(4)]
    return tables + others, jnp.stack(blocks).astype(I32)


def on_device(user_rows, item_table, observed_items, counts, item_row):
    exchange = lambda x, axes: lax.all_to_all(x, axes, 0, 0, tiled=True)
    group = USERS_DEV // N_DIM
    users = exchange(user_rows.reshape(N_DIM, group, BLOCK), DIM)
    tables, blocks = gather_dims(item_table)
    diag = dot(item_table, item_table, 0, 0)
    diag = exchange(diag.reshape(N_ROWS, BLOCK // N_ROWS, BLOCK), ROWS)
    pos, req = call(
        index_kernel, (shape((SLOTS, 1), I32), shape((1, SLOTS), I32)), 2, 3 << 30, 4 << 20
    )(observed_items.reshape(SLOTS, 1), item_row.reshape(256, 128))
    req = exchange(req.reshape(N_ROWS, PER), ROWS)
    users = exchange(jnp.broadcast_to(users[None], (8, N_DIM, group, BLOCK)), "z")
    diag = jnp.sum(diag, axis=0)
    diag = exchange(jnp.broadcast_to(diag[None], (N_ROWS, BLOCK // N_ROWS, BLOCK)), ROWS)
    users = exchange(jnp.broadcast_to(users[None], (4, 8, N_DIM, group, BLOCK)), "x")
    users = users.transpose(2, 0, 1, 3, 4).reshape(N_DIM, BLOCK, BLOCK)
    rows = call(pick_kernel, shape((SLOTS, BLOCK), BF16), 2, 1 << 30, 4 << 20)(
        req.reshape(SLOTS, 1), item_table
    )
    came = exchange(rows.reshape(N_ROWS, PER, BLOCK), ROWS).reshape(SLOTS, BLOCK)
    times = call(
        product_kernel,
        shape((BLOCK, N_DIM * BLOCK), F32),
        2 + N_DIM,
        4 << 30,
        8 << 20,
        in_specs=[SMEM] + [VMEM] * (1 + N_DIM),
    )(blocks, users, *tables)
    times = exchange(times.reshape(4, 8, group, N_DIM * BLOCK), "x")
    inverse = call(
        inverse_kernel,
        shape((BLOCK, BLOCK), F32),
        1,
        8 << 30,
        16 << 20,
        scratch=[pltpu.VMEM((BLOCK, BLOCK), F32)],
    )(diag.reshape(BLOCK, BLOCK))
    counts = counts.reshape(1, USERS_DEV)
    fetched, pred = call(
        place_kernel,
        (shape((SLOTS, BLOCK), BF16), shape((LIST, USERS_DEV), F32)),
        3,
        3 << 30,
        8 << 20,
    )(pos, came, user_rows)
    pred = exchange(jnp.broadcast_to(pred[None], (N_DIM, LIST, USERS_DEV)), DIM)
    times = exchange(jnp.sum(times, axis=0), "z")
    inner = call(
        inner_kernel,
        shape((LIST, LIST, USERS_DEV), F32),
        3,
        3 << 30,
        16 << 20,
        scratch=[
            pltpu.VMEM((SLOTS, 128), F32),
            pltpu.VMEM((LIST, LIST, USERS_DEV), F32),
        ],
    )(fetched, inverse, counts)
    times = jnp.sum(times, axis=0).reshape(group, N_DIM, BLOCK).transpose(1, 0, 2)
    times = exchange(times, DIM).reshape(USERS_DEV, BLOCK)
    return call(final_kernel, shape((USERS_DEV, BLOCK), F32), 7, 1 << 30, 4 << 20)(
        fetched, inverse, inner, counts, pred, user_rows, times
    )


def solution(mesh):
    fine = Mesh(mesh.devices.reshape(4, 2, 4, 8), ("y", "core", "x", "z"))
    in_specs = (P(ROWS, DIM), P(ROWS, DIM), P(ROWS, None), P(ROWS), P())
    return jax.shard_map(
        on_device, mesh=fine, in_specs=in_specs, out_specs=P(ROWS, DIM), check_vma=False
    )
```

```python
import jax
import jax.numpy as jnp
from jax import lax
from jax.experimental import pallas as pl
from jax.experimental.pallas import tpu as pltpu
from jax.sharding import Mesh, PartitionSpec as P

F32 = jnp.float32
BF16 = jnp.bfloat16
I32 = jnp.int32
ROWS = ("x", "z")
DIM = ("y", "core")
BLOCK = 256
LIST = 32
USERS_DEV = 64
SLOTS = USERS_DEV * LIST
ITEM_DEV = 1024
N_ROWS = 32
N_DIM = 8
PER = SLOTS // N_ROWS
CHUNK = 256
CHUNKS = SLOTS // CHUNK
WEIGHT = 32.0 / 32768.0
VMEM = pl.BlockSpec(memory_space=pltpu.VMEM)
SMEM = pl.BlockSpec(memory_space=pltpu.SMEM)


def iota(shape, dim):
    return lax.broadcasted_iota(I32, shape, dim)


def dot(a, b, ca=1, cb=0):
    return lax.dot_general(a, b, (((ca,), (cb,)), ((), ())), preferred_element_type=F32)


def split(a):
    top = a.astype(BF16)
    rest = a - top.astype(F32)
    mid = rest.astype(BF16)
    low = (rest - mid.astype(F32)).astype(BF16)
    return top, mid, low


def dot_split(a, b, ca=1, cb=0):
    a0, a1, a2 = a
    b0, b1, b2 = b
    small = dot(a2, b0, ca, cb) + dot(a0, b2, ca, cb) + dot(a1, b1, ca, cb)
    return (small + (dot(a1, b0, ca, cb) + dot(a0, b1, ca, cb))) + dot(a0, b0, ca, cb)


def one_hot(column, width):
    hit = iota((column.shape[0], width), 1) == column
    return jnp.where(hit, 1.0, 0.0).astype(BF16)


def call(kernel, out_shape, n_in, flops, nbytes, scratch=(), in_specs=None):
    multi = isinstance(out_shape, (tuple, list))
    return pl.pallas_call(
        kernel,
        out_shape=out_shape,
        in_specs=in_specs or [VMEM] * n_in,
        out_specs=[VMEM] * len(out_shape) if multi else VMEM,
        scratch_shapes=list(scratch),
        compiler_params=pltpu.CompilerParams(vmem_limit_bytes=20 << 20),
        cost_estimate=pl.CostEstimate(flops=flops, bytes_accessed=nbytes, transcendentals=0),
    )


def chunk_column(array, c):
    width = array.shape[0]
    step = CHUNK // width
    return jnp.concatenate(
        [array[:, c * step + i : c * step + i + 1] for i in range(step)], axis=0
    )


def index_kernel(ids_ref, table_ref, diag_ref, pos_ref, sent_ref):
    table = table_ref[...]
    table_hi = (table >> 8).astype(F32).astype(BF16)
    table_lo = (table & 255).astype(F32).astype(BF16)
    lane = iota((CHUNK, 128), 1)
    before = jnp.where(
        iota((CHUNK, CHUNK), 0) > iota((CHUNK, CHUNK), 1), 1.0, 0.0
    ).astype(BF16)
    totals = jnp.zeros((1, 128), F32)
    asked = jnp.zeros((128, 128), F32)
    places = jnp.zeros((CHUNK, 128), I32)
    ids_all = ids_ref[...]
    for c in range(CHUNKS):
        ids = chunk_column(ids_all, c)
        picked = one_hot(ids >> 7, 256)
        values = dot(picked, table_hi) * 256.0 + dot(picked, table_lo)
        row = jnp.sum(jnp.where(lane == (ids & 127), values, 0.0), axis=1, keepdims=True)
        row = row.astype(I32)
        member = jnp.where(lane == (row >> 10), 1.0, 0.0)
        ranks = dot(before, member.astype(BF16)) + totals
        rank = jnp.sum(member * ranks, axis=1, keepdims=True).astype(I32)
        totals = totals + jnp.sum(member, axis=0, keepdims=True)
        places = jnp.where(lane == c, (row >> 10) * PER + rank, places)
        ranked = one_hot(rank, 128)
        high = member * ((row >> 5) & 31).astype(F32)
        low = member * (row & 31).astype(F32)
        asked = asked + dot(high.astype(BF16), ranked, 0, 0) * 32.0
        asked = asked + dot(low.astype(BF16), ranked, 0, 0)
    pos_ref[...] = places
    sent_ref[...] = jnp.zeros(sent_ref.shape, F32)
    sent_ref[:, :8, :] = diag_ref[...]
    for k in range(N_ROWS):
        sent_ref[k, 8:9, :128] = asked[k : k + 1, :]


def pick_kernel(came_ref, table_ref, rows_ref, diag_ref):
    table = table_ref[...]
    diag = came_ref[0, :8, :]
    for r in range(1, N_ROWS):
        diag = diag + came_ref[r, :8, :]
    diag_ref[...] = jnp.broadcast_to(diag[None], diag_ref.shape)
    asked = jnp.concatenate([came_ref[r, 8:9, :128] for r in range(N_ROWS)], axis=0)
    asked = jnp.transpose(asked).astype(I32)
    asked = asked[:PER, :]
    for c in range(CHUNKS):
        column = chunk_column(asked, c)
        rows = dot(one_hot(column, ITEM_DEV), table).astype(BF16)
        rows_ref[c * CHUNK : (c + 1) * CHUNK, :] = rows


def place_kernel(pos_ref, came_ref, users_ref, fetched_ref, pred_ref):
    came = came_ref[...]
    users = users_ref[...]
    lane = iota((LIST, USERS_DEV), 1)
    pred = jnp.zeros((LIST, USERS_DEV), F32)
    for c in range(CHUNKS):
        part = slice(c * CHUNK, (c + 1) * CHUNK)
        rows = dot(one_hot(pos_ref[:, c : c + 1], SLOTS), came).astype(BF16)
        fetched_ref[part, :] = rows
        cross = dot(rows, users, 1, 1)
        for i in range(CHUNK // LIST):
            user = c * (CHUNK // LIST) + i
            pred = pred + jnp.where(lane == user, cross[i * LIST : (i + 1) * LIST, :], 0.0)
    pred_ref[...] = pred


def product_kernel(block_ref, *refs):
    users_refs, tables = refs[:4], refs[4 : 4 + N_DIM]
    out_refs, held, sems = refs[4 + N_DIM : -2], refs[-2], refs[-1]
    quarter = BLOCK // 4
    copies = [pltpu.make_async_copy(tables[i], held.at[i], sems.at[i]) for i in range(N_DIM)]
    for copy in copies:
        copy.start()
    scores = jnp.zeros((BLOCK, ITEM_DEV), F32)
    for i in range(N_DIM):
        block = block_ref[i]
        users = [u[:, block].astype(F32).reshape(quarter, BLOCK) for u in users_refs]
        users = jnp.concatenate(users, axis=0).astype(BF16)
        copies[i].wait()
        scores = scores + dot(users, held[i], 1, 1)
    s0, s1, s2 = split(scores)
    for i in range(N_DIM):
        table = held[i]
        times = (dot(s2, table) + dot(s1, table)) + dot(s0, table)
        for n, out_ref in enumerate(out_refs):
            part = times[n * quarter : (n + 1) * quarter]
            out_ref[:, block_ref[i]] = part.reshape(8, quarter // 8, BLOCK)


def sweep(work):
    size = 128
    lane = iota((8, size), 1)
    wide = iota((size, size), 1)

    def at_lane(row, k):
        return jnp.take_along_axis(row, jnp.full((8, size), k, I32), axis=1)

    def load(k):
        return jnp.broadcast_to(work[pl.ds(k, 1), :], (8, size))

    def column(row):
        return jnp.transpose(jnp.broadcast_to(row[:1], (size, size)))

    def step(n, rows):
        row0, raw1 = rows
        k = 2 * n
        after = jnp.minimum(k + 2, size - 2)
        old2 = load(after)
        old3 = load(after + 1)
        inv0 = 1.0 / at_lane(row0, k)
        c01 = at_lane(row0, k + 1)
        a2, a3 = at_lane(row0, after), at_lane(row0, after + 1)
        b2, b3 = at_lane(raw1, after), at_lane(raw1, after + 1)
        low = c01 * inv0
        inv1 = 1.0 / (at_lane(raw1, k + 1) - c01 * low)
        w0 = row0 * inv0
        row1 = jnp.where(lane == k, low, raw1 - c01 * w0)
        w1 = row1 * inv1
        b2 = b2 - low * a2
        b3 = b3 - low * a3

        def advance(old, a, b):
            once = jnp.where(lane == k, a * inv0, old - a * w0)
            return jnp.where(lane == k + 1, b * inv1, once - b * w1)

        next0 = advance(old2, a2, b2)
        next1 = advance(old3, a3, b3)
        col0, col1 = column(row0), column(row1)
        new = jnp.where(wide == k, col0 * inv0[:1], work[...] - col0 * w0[:1])
        work[...] = jnp.where(wide == k + 1, col1 * inv1[:1], new - col1 * w1[:1])
        done0 = jnp.where(lane == k, -inv0, w0)
        done0 = jnp.where(lane == k + 1, low * inv1, done0 - low * w1)
        work[pl.ds(k, 1), :] = done0[:1]
        work[pl.ds(k + 1, 1), :] = jnp.where(lane == k + 1, -inv1, w1)[:1]
        return next0, next1

    lax.fori_loop(0, size // 2, step, (load(0), load(1)))
    return -work[...]


def inverse_kernel(diag_ref, out_ref, work):
    half = BLOCK // 2
    eye = jnp.where(iota((half, half), 0) == iota((half, half), 1), 1.0, 0.0)
    upper = WEIGHT * diag_ref[:half, half:]
    work[...] = WEIGHT * diag_ref[:half, :half] + eye
    lead = sweep(work)
    lead_split = split(lead)
    upper_split = split(upper)
    mixed = dot_split(lead_split, upper_split)
    mixed_split = split(mixed)
    work[...] = WEIGHT * diag_ref[half:, half:] + eye - dot_split(upper_split, mixed_split, 0, 0)
    rest = sweep(work)
    cross = dot_split(mixed_split, split(rest))
    out_ref[:half, :half] = lead + dot_split(split(cross), mixed_split, 1, 1)
    out_ref[:half, half:] = -cross
    out_ref[half:, :half] = -jnp.transpose(cross)
    out_ref[half:, half:] = rest


def inner_kernel(fetched_ref, inverse_ref, counts_ref, out_ref, folded, work):
    i0, i1, i2 = split(inverse_ref[...])
    same = iota((CHUNK, CHUNK), 0) // LIST == iota((CHUNK, CHUNK), 1) // LIST

    def chunk(c, carry):
        part = pl.ds(pl.multiple_of(c * CHUNK, CHUNK), CHUNK)
        rows = fetched_ref[part, :]
        scaled = (dot(rows, i2) + dot(rows, i1)) + dot(rows, i0)
        s0, s1, s2 = split(scaled)
        cross = (dot(s2, rows, 1, 1) + dot(s1, rows, 1, 1)) + dot(s0, rows, 1, 1)
        cross = jnp.where(same, cross, 0.0)
        both = cross[:, :128] + cross[:, 128:]
        both = both + pltpu.roll(both, 64, 1)
        folded[part, :] = both + pltpu.roll(both, 32, 1)
        return carry

    lax.fori_loop(0, CHUNKS, chunk, 0, unroll=2)
    slot = iota((LIST, USERS_DEV), 0)
    live = jnp.where(slot < counts_ref[...], 1.0, 0.0)
    for a in range(LIST):
        mine = jnp.transpose(folded[pl.ds(a, USERS_DEV, stride=LIST), :])[:LIST, :]
        work[a] = mine * (live * live[a : a + 1, :]) + jnp.where(slot == a, 1.0, 0.0)

    def step(k, carry):
        row = work[k]
        pivot = work[k, pl.ds(k, 1), :]
        inv = 1.0 / pivot
        scaled = row * inv
        here = slot == k
        for a in range(LIST):
            factor = row[a : a + 1, :]
            work[a] = jnp.where(here, factor * inv, work[a] - factor * scaled)
        work[k] = jnp.where(here, -inv, scaled)
        return carry

    lax.fori_loop(0, LIST, step, 0)
    out_ref[...] = -work[...]


def spread(values):
    flat = jnp.transpose(values)
    wide = jnp.concatenate([flat] * 4, axis=1)
    wide = jnp.concatenate([wide] * (SLOTS // 128), axis=1)
    own = iota((USERS_DEV, SLOTS), 1) // LIST == iota((USERS_DEV, SLOTS), 0)
    return jnp.where(own, wide, 0.0)


def weigh(values, fetched):
    s0, s1, s2 = split(spread(values))
    return (dot(s2, fetched) + dot(s1, fetched)) + dot(s0, fetched)


def final_kernel(
    fetched_ref, inverse_ref, inner_ref, counts_ref, users_ref, times_ref, *refs
):
    pred_refs, out_ref = refs[:-1], refs[-1]
    fetched = fetched_ref[...]
    inverse = split(inverse_ref[...])
    own = users_ref[...].astype(F32)
    slot = iota((LIST, USERS_DEV), 0)
    lane = iota((LIST, USERS_DEV), 1)
    live = jnp.where(slot < counts_ref[...], 1.0, 0.0)
    pred = pred_refs[0][...]
    for ref in pred_refs[1:]:
        pred = pred + ref[...]
    residual = live * (pred - 1.0)
    times = times_ref[0]
    for i in range(1, 8):
        times = times + times_ref[i]
    gradient = weigh(residual, fetched) + WEIGHT * times + own
    scaled = dot_split(split(gradient), inverse)
    y0, y1, y2 = split(scaled)
    cross = (dot(fetched, y2, 1, 1) + dot(fetched, y1, 1, 1)) + dot(fetched, y0, 1, 1)
    projected = jnp.zeros((LIST, USERS_DEV), F32)
    for user in range(USERS_DEV):
        projected = projected + jnp.where(
            lane == user, cross[user * LIST : (user + 1) * LIST, :], 0.0
        )
    projected = projected * live
    weights = jnp.zeros((LIST, USERS_DEV), F32)
    for a in range(LIST):
        weights = weights + inner_ref[a] * projected[a : a + 1, :]
    weights = weights * live
    back = dot_split(split(weigh(weights, fetched)), inverse)
    out_ref[...] = own - (scaled - back)


def shape(dims, dtype):
    return jax.ShapeDtypeStruct(dims, dtype)


def shift(x, axis, by):
    size = {"x": 4, "y": 4, "core": 2}[axis]
    return lax.ppermute(x, axis, [(i, (i + by) % size) for i in range(size)])


def gather_dims(table):
    tables = [table] + [shift(table, "y", 4 - i) for i in (1, 3, 2)]
    tables = tables + [shift(t, "core", 1) for t in tables]
    y = lax.axis_index("y")
    core = lax.axis_index("core")
    blocks = [((y + i) % 4) * 2 + (core + j) % 2 for j in (0, 1) for i in (0, 1, 3, 2)]
    return tables, jnp.stack(blocks).astype(I32)


def exchange(x, axes):
    return lax.all_to_all(x, axes, 0, 0, tiled=True)


def body(user_rows, item_table, observed_items, counts, item_row):
    group = USERS_DEV // N_DIM
    slice_rows = BLOCK // N_ROWS
    users = user_rows.reshape(1, N_DIM, group, BLOCK)
    users = jnp.broadcast_to(users, (8, N_DIM, group, BLOCK))
    users = exchange(users.reshape(8 * N_DIM, group, BLOCK), ("z",) + DIM)
    tables, blocks = gather_dims(item_table)
    diag = dot(item_table, item_table, 0, 0).reshape(N_ROWS, slice_rows, BLOCK)
    pos, sent = call(
        index_kernel, (shape((CHUNK, 128), I32), shape((N_ROWS, 16, BLOCK), F32)), 3, 1 << 30, 4 << 20
    )(observed_items.T, item_row.reshape(256, 128), diag)
    came = exchange(sent, ROWS)
    users = users.reshape(8, N_DIM, group, BLOCK)
    users = [users] + [shift(users, "x", 4 - i) for i in range(1, 4)]
    rows, diag = call(
        pick_kernel,
        (shape((SLOTS, BLOCK), BF16), shape((N_ROWS, slice_rows, BLOCK), F32)),
        2,
        1 << 30,
        4 << 20,
    )(came, item_table)
    came = exchange(rows.reshape(N_ROWS, PER, BLOCK), ROWS).reshape(SLOTS, BLOCK)
    diag = exchange(diag, ROWS)
    times = call(
        product_kernel,
        [shape((8, N_DIM, group, BLOCK), F32)] * 4,
        5 + len(tables),
        4 << 30,
        8 << 20,
        scratch=[
            pltpu.VMEM((N_DIM, ITEM_DEV, BLOCK), BF16),
            pltpu.SemaphoreType.DMA((N_DIM,)),
        ],
        in_specs=[SMEM] + [VMEM] * 4 + [pl.BlockSpec(memory_space=pl.ANY)] * N_DIM,
    )(blocks, *users, *tables)
    times = [times[0]] + [shift(times[i], "x", i) for i in range(1, 4)]
    inverse = call(
        inverse_kernel,
        shape((BLOCK, BLOCK), F32),
        1,
        4 << 30,
        8 << 20,
        scratch=[pltpu.VMEM((BLOCK // 2, BLOCK // 2), F32)],
    )(diag.reshape(BLOCK, BLOCK))
    counts = counts.reshape(1, USERS_DEV)
    fetched, pred = call(
        place_kernel,
        (shape((SLOTS, BLOCK), BF16), shape((LIST, USERS_DEV), F32)),
        3,
        3 << 30,
        8 << 20,
    )(pos, came, user_rows)
    pred = pred + shift(pred, "core", 1)
    pred = [pred] + [shift(pred, "y", i) for i in range(1, 4)]
    times = (times[0] + times[1]) + (times[2] + times[3])
    times = exchange(times.reshape(8 * N_DIM, group, BLOCK), ("z",) + DIM)
    inner = call(
        inner_kernel,
        shape((LIST, LIST, USERS_DEV), F32),
        3,
        3 << 30,
        16 << 20,
        scratch=[
            pltpu.VMEM((SLOTS, 128), F32),
            pltpu.VMEM((LIST, LIST, USERS_DEV), F32),
        ],
    )(fetched, inverse, counts)
    times = times.reshape(8, USERS_DEV, BLOCK)
    return call(final_kernel, shape((USERS_DEV, BLOCK), F32), 10, 1 << 30, 4 << 20)(
        fetched, inverse, inner, counts, user_rows, times, *pred
    )


def solution(mesh):
    fine = Mesh(mesh.devices.reshape(4, 2, 4, 8), ("y", "core", "x", "z"))
    in_specs = (P(ROWS, DIM), P(ROWS, DIM), P(ROWS, None), P(ROWS), P())
    return jax.shard_map(
        body, mesh=fine, in_specs=in_specs, out_specs=P(ROWS, DIM), check_vma=False
    )
```

```python
import jax
import jax.numpy as jnp
from jax import lax
from jax.experimental import pallas as pl
from jax.experimental.pallas import tpu as pltpu
from jax.sharding import Mesh, PartitionSpec as P

F32 = jnp.float32
BF16 = jnp.bfloat16
I32 = jnp.int32
ROWS = ("x", "z")
DIM = ("y", "core")
BLOCK = 256
LIST = 32
USERS_DEV = 64
SLOTS = USERS_DEV * LIST
ITEM_DEV = 1024
N_ROWS = 32
N_DIM = 8
PER = SLOTS // N_ROWS
CHUNK = 256
CHUNKS = SLOTS // CHUNK
WEIGHT = 32.0 / 32768.0
VMEM = pl.BlockSpec(memory_space=pltpu.VMEM)
SMEM = pl.BlockSpec(memory_space=pltpu.SMEM)


def iota(shape, dim):
    return lax.broadcasted_iota(I32, shape, dim)


def dot(a, b, ca=1, cb=0):
    return lax.dot_general(a, b, (((ca,), (cb,)), ((), ())), preferred_element_type=F32)


def split(a):
    top = a.astype(BF16)
    rest = a - top.astype(F32)
    mid = rest.astype(BF16)
    low = (rest - mid.astype(F32)).astype(BF16)
    return top, mid, low


def dot_split(a, b, ca=1, cb=0):
    a0, a1, a2 = a
    b0, b1, b2 = b
    small = dot(a2, b0, ca, cb) + dot(a0, b2, ca, cb) + dot(a1, b1, ca, cb)
    return (small + (dot(a1, b0, ca, cb) + dot(a0, b1, ca, cb))) + dot(a0, b0, ca, cb)


def one_hot(column, width):
    hit = iota((column.shape[0], width), 1) == column
    return jnp.where(hit, 1.0, 0.0).astype(BF16)


def call(kernel, out_shape, n_in, flops, nbytes, scratch=(), in_specs=None):
    multi = isinstance(out_shape, (tuple, list))
    return pl.pallas_call(
        kernel,
        out_shape=out_shape,
        in_specs=in_specs or [VMEM] * n_in,
        out_specs=[VMEM] * len(out_shape) if multi else VMEM,
        scratch_shapes=list(scratch),
        compiler_params=pltpu.CompilerParams(vmem_limit_bytes=20 << 20),
        cost_estimate=pl.CostEstimate(flops=flops, bytes_accessed=nbytes, transcendentals=0),
    )


def chunk_column(array, c):
    width = array.shape[0]
    step = CHUNK // width
    return jnp.concatenate(
        [array[:, c * step + i : c * step + i + 1] for i in range(step)], axis=0
    )


def index_kernel(ids_ref, table_ref, diag_ref, pos_ref, sent_ref):
    table = table_ref[...]
    table_hi = (table >> 8).astype(F32).astype(BF16)
    table_lo = (table & 255).astype(F32).astype(BF16)
    lane = iota((CHUNK, 128), 1)
    before = jnp.where(
        iota((CHUNK, CHUNK), 0) > iota((CHUNK, CHUNK), 1), 1.0, 0.0
    ).astype(BF16)
    totals = jnp.zeros((1, 128), F32)
    asked = jnp.zeros((128, 128), F32)
    places = jnp.zeros((CHUNK, 128), I32)
    ids_all = ids_ref[...]
    for c in range(CHUNKS):
        ids = chunk_column(ids_all, c)
        picked = one_hot(ids >> 7, 256)
        values = dot(picked, table_hi) * 256.0 + dot(picked, table_lo)
        row = jnp.sum(jnp.where(lane == (ids & 127), values, 0.0), axis=1, keepdims=True)
        row = row.astype(I32)
        member = jnp.where(lane == (row >> 10), 1.0, 0.0)
        ranks = dot(before, member.astype(BF16)) + totals
        rank = jnp.sum(member * ranks, axis=1, keepdims=True).astype(I32)
        totals = totals + jnp.sum(member, axis=0, keepdims=True)
        places = jnp.where(lane == c, (row >> 10) * PER + rank, places)
        ranked = one_hot(rank, 128)
        high = member * ((row >> 5) & 31).astype(F32)
        low = member * (row & 31).astype(F32)
        asked = asked + dot(high.astype(BF16), ranked, 0, 0) * 32.0
        asked = asked + dot(low.astype(BF16), ranked, 0, 0)
    pos_ref[...] = places
    sent_ref[...] = jnp.zeros(sent_ref.shape, F32)
    sent_ref[:, :, :BLOCK] = diag_ref[...]
    for k in range(N_ROWS):
        sent_ref[k, 0:1, BLOCK:] = asked[k : k + 1, :]


def pick_kernel(came_ref, table_ref, rows_ref, diag_ref):
    table = table_ref[...]
    diag = came_ref[0, :, :BLOCK]
    for r in range(1, N_ROWS):
        diag = diag + came_ref[r, :, :BLOCK]
    diag_ref[...] = jnp.broadcast_to(diag[None], diag_ref.shape)
    asked = jnp.concatenate([came_ref[r, 0:1, BLOCK:] for r in range(N_ROWS)], axis=0)
    asked = jnp.transpose(asked).astype(I32)
    asked = asked[:PER, :]
    for c in range(CHUNKS):
        column = chunk_column(asked, c)
        rows = dot(one_hot(column, ITEM_DEV), table).astype(BF16)
        rows_ref[c * CHUNK : (c + 1) * CHUNK, :] = rows


def place_kernel(pos_ref, came_ref, users_ref, fetched_ref, pred_ref):
    came = came_ref[...]
    users = users_ref[...]
    lane = iota((LIST, USERS_DEV), 1)
    pred = jnp.zeros((LIST, USERS_DEV), F32)
    for c in range(CHUNKS):
        part = slice(c * CHUNK, (c + 1) * CHUNK)
        rows = dot(one_hot(pos_ref[:, c : c + 1], SLOTS), came).astype(BF16)
        fetched_ref[part, :] = rows
        cross = dot(rows, users, 1, 1)
        for i in range(CHUNK // LIST):
            user = c * (CHUNK // LIST) + i
            pred = pred + jnp.where(lane == user, cross[i * LIST : (i + 1) * LIST, :], 0.0)
    pred_ref[...] = pred


def product_kernel(block_ref, *refs):
    users_refs, tables = refs[:4], refs[4 : 4 + N_DIM]
    out_refs, held, sems = refs[4 + N_DIM : -2], refs[-2], refs[-1]
    quarter = BLOCK // 4
    copies = [pltpu.make_async_copy(tables[i], held.at[i], sems.at[i]) for i in range(N_DIM)]
    for copy in copies:
        copy.start()
    scores = jnp.zeros((BLOCK, ITEM_DEV), F32)
    for i in range(N_DIM):
        block = block_ref[i]
        users = [u[:, block].astype(F32).reshape(quarter, BLOCK) for u in users_refs]
        users = jnp.concatenate(users, axis=0).astype(BF16)
        copies[i].wait()
        scores = scores + dot(users, held[i], 1, 1)
    s0, s1, s2 = split(scores)
    for i in range(N_DIM):
        table = held[i]
        times = (dot(s2, table) + dot(s1, table)) + dot(s0, table)
        for n, out_ref in enumerate(out_refs):
            part = times[n * quarter : (n + 1) * quarter]
            out_ref[:, block_ref[i]] = part.reshape(8, quarter // 8, BLOCK)


def sweep(start):
    size, group = 128, 4
    lane = iota((size, size), 1)
    sub = iota((size, size), 0)
    row_lane = iota((1, size), 1)

    def eight(n, a):
        for k0 in range(0, 8, group):
            cols = [jnp.broadcast_to(a[:, k : k + 1], (size, size)) for k in range(k0, k0 + group)]
            rows = [a[k : k + 1, :] for k in range(k0, k0 + group)]
            for j in range(group):
                k = k0 + j
                inv = 1.0 / cols[j][k : k + 1, :]
                scaled = rows[j] * inv
                for m in range(j + 1, group):
                    low = cols[m][k : k + 1, :] * inv
                    factor = cols[j][k0 + m : k0 + m + 1, :]
                    cols[m] = jnp.where(sub == k, low, cols[m] - cols[j] * low)
                    rows[m] = jnp.where(row_lane == k, factor * inv, rows[m] - factor * scaled)
                a = jnp.where(lane == k, cols[j] * inv, a - cols[j] * scaled)
                a = jnp.where(sub == k, jnp.where(row_lane == k, -inv, scaled), a)
        a = pltpu.roll(a, size - 8, 1)
        return jnp.concatenate([a[8:], a[:8]], axis=0)

    return -lax.fori_loop(0, size // 8, eight, start)


def inverse_kernel(diag_ref, out_ref):
    half = BLOCK // 2
    eye = jnp.where(iota((half, half), 0) == iota((half, half), 1), 1.0, 0.0)
    upper = split(WEIGHT * diag_ref[:half, half:])
    lead = sweep(WEIGHT * diag_ref[:half, :half] + eye)
    mixed = split(dot_split(split(lead), upper))
    rest = WEIGHT * diag_ref[half:, half:] + eye - dot_split(upper, mixed, 0, 0)
    rest = sweep(rest)
    cross = dot_split(mixed, split(rest))
    out_ref[:half, :half] = lead + dot_split(split(cross), mixed, 1, 1)
    out_ref[:half, half:] = -cross
    out_ref[half:, :half] = -jnp.transpose(cross)
    out_ref[half:, half:] = rest


def inner_kernel(fetched_ref, inverse_ref, counts_ref, out_ref, folded, work):
    i0, i1, i2 = split(inverse_ref[...])
    same = iota((CHUNK, CHUNK), 0) // LIST == iota((CHUNK, CHUNK), 1) // LIST

    def chunk(c, carry):
        part = pl.ds(pl.multiple_of(c * CHUNK, CHUNK), CHUNK)
        rows = fetched_ref[part, :]
        scaled = (dot(rows, i2) + dot(rows, i1)) + dot(rows, i0)
        s0, s1, s2 = split(scaled)
        cross = (dot(s2, rows, 1, 1) + dot(s1, rows, 1, 1)) + dot(s0, rows, 1, 1)
        cross = jnp.where(same, cross, 0.0)
        both = cross[:, :128] + cross[:, 128:]
        both = both + pltpu.roll(both, 64, 1)
        folded[part, :] = both + pltpu.roll(both, 32, 1)
        return carry

    lax.fori_loop(0, CHUNKS, chunk, 0, unroll=4)
    slot = iota((LIST, USERS_DEV), 0)
    live = jnp.where(slot < counts_ref[...], 1.0, 0.0)
    for a in range(LIST):
        mine = jnp.transpose(folded[pl.ds(a, USERS_DEV, stride=LIST), :])[:LIST, :]
        work[a] = mine * (live * live[a : a + 1, :]) + jnp.where(slot == a, 1.0, 0.0)

    def step(k, carry):
        row = work[k]
        pivot = work[k, pl.ds(k, 1), :]
        inv = 1.0 / pivot
        scaled = row * inv
        here = slot == k
        for a in range(LIST):
            factor = row[a : a + 1, :]
            work[a] = jnp.where(here, factor * inv, work[a] - factor * scaled)
        work[k] = jnp.where(here, -inv, scaled)
        return carry

    lax.fori_loop(0, LIST, step, 0)
    out_ref[...] = -work[...]


def spread(values):
    flat = jnp.transpose(values)
    wide = jnp.concatenate([flat] * 4, axis=1)
    wide = jnp.concatenate([wide] * (SLOTS // 128), axis=1)
    own = iota((USERS_DEV, SLOTS), 1) // LIST == iota((USERS_DEV, SLOTS), 0)
    return jnp.where(own, wide, 0.0)


def weigh(values, fetched):
    s0, s1, s2 = split(spread(values))
    return (dot(s2, fetched) + dot(s1, fetched)) + dot(s0, fetched)


def final_kernel(
    fetched_ref, inverse_ref, inner_ref, counts_ref, users_ref, times_ref, *refs
):
    pred_refs, out_ref = refs[:-1], refs[-1]
    fetched = fetched_ref[...]
    inverse = split(inverse_ref[...])
    own = users_ref[...].astype(F32)
    slot = iota((LIST, USERS_DEV), 0)
    lane = iota((LIST, USERS_DEV), 1)
    live = jnp.where(slot < counts_ref[...], 1.0, 0.0)
    pred = pred_refs[0][...]
    for ref in pred_refs[1:]:
        pred = pred + ref[...]
    residual = live * (pred - 1.0)
    times = times_ref[0]
    for i in range(1, 8):
        times = times + times_ref[i]
    gradient = weigh(residual, fetched) + WEIGHT * times + own
    scaled = dot_split(split(gradient), inverse)
    y0, y1, y2 = split(scaled)
    cross = (dot(fetched, y2, 1, 1) + dot(fetched, y1, 1, 1)) + dot(fetched, y0, 1, 1)
    projected = jnp.zeros((LIST, USERS_DEV), F32)
    for user in range(USERS_DEV):
        projected = projected + jnp.where(
            lane == user, cross[user * LIST : (user + 1) * LIST, :], 0.0
        )
    projected = projected * live
    weights = jnp.zeros((LIST, USERS_DEV), F32)
    for a in range(LIST):
        weights = weights + inner_ref[a] * projected[a : a + 1, :]
    weights = weights * live
    back = dot_split(split(weigh(weights, fetched)), inverse)
    out_ref[...] = own - (scaled - back)


def shape(dims, dtype):
    return jax.ShapeDtypeStruct(dims, dtype)


def shift(x, axis, by):
    size = {"x": 4, "y": 4, "core": 2}[axis]
    return lax.ppermute(x, axis, [(i, (i + by) % size) for i in range(size)])


def gather_dims(table):
    tables = [table] + [shift(table, "y", 4 - i) for i in (1, 3)]
    tables = tables + [shift(table, "y", 2)]
    tables = tables + [shift(t, "core", 1) for t in tables]
    y = lax.axis_index("y")
    core = lax.axis_index("core")
    blocks = [((y + i) % 4) * 2 + (core + j) % 2 for j in (0, 1) for i in (0, 1, 3, 2)]
    return tables, jnp.stack(blocks).astype(I32)


def exchange(x, axes):
    return lax.all_to_all(x, axes, 0, 0, tiled=True)


def body(user_rows, item_table, observed_items, counts, item_row):
    group = USERS_DEV // N_DIM
    slice_rows = BLOCK // N_ROWS
    users = user_rows.reshape(1, N_DIM, group, BLOCK)
    users = jnp.broadcast_to(users, (8, N_DIM, group, BLOCK))
    users = exchange(users.reshape(8 * N_DIM, group, BLOCK), ("z",) + DIM)
    tables, blocks = gather_dims(item_table)
    diag = dot(item_table, item_table, 0, 0).reshape(N_ROWS, slice_rows, BLOCK)
    pos, sent = call(
        index_kernel, (shape((CHUNK, 128), I32), shape((N_ROWS, 8, BLOCK + 128), F32)), 3, 1 << 30, 4 << 20
    )(observed_items.T, item_row.reshape(256, 128), diag)
    came = exchange(sent, ROWS)
    users = users.reshape(8, N_DIM, group, BLOCK)
    users = [users] + [shift(users, "x", 4 - i) for i in range(1, 4)]
    rows, diag = call(
        pick_kernel,
        (shape((SLOTS, BLOCK), BF16), shape((N_ROWS, slice_rows, BLOCK), F32)),
        2,
        1 << 30,
        4 << 20,
    )(came, item_table)
    came = exchange(rows.reshape(N_ROWS, PER, BLOCK), ROWS).reshape(SLOTS, BLOCK)
    diag = exchange(diag, ROWS)
    times = call(
        product_kernel,
        [shape((8, N_DIM, group, BLOCK), F32)] * 4,
        5 + len(tables),
        4 << 30,
        8 << 20,
        scratch=[
            pltpu.VMEM((N_DIM, ITEM_DEV, BLOCK), BF16),
            pltpu.SemaphoreType.DMA((N_DIM,)),
        ],
        in_specs=[SMEM] + [VMEM] * 4 + [pl.BlockSpec(memory_space=pl.ANY)] * N_DIM,
    )(blocks, *users, *tables)
    far = shift(times[2], "x", 2)
    times = [times[0], far] + [shift(times[i], "x", i) for i in (1, 3)]
    inverse = call(
        inverse_kernel, shape((BLOCK, BLOCK), F32), 1, 4 << 30, 8 << 20
    )(diag.reshape(BLOCK, BLOCK))
    counts = counts.reshape(1, USERS_DEV)
    fetched, pred = call(
        place_kernel,
        (shape((SLOTS, BLOCK), BF16), shape((LIST, USERS_DEV), F32)),
        3,
        3 << 30,
        8 << 20,
    )(pos, came, user_rows)
    pred = pred + shift(pred, "core", 1)
    pred = [pred] + [shift(pred, "y", i) for i in range(1, 4)]
    times = (times[0] + times[1]) + (times[2] + times[3])
    times = exchange(times.reshape(8 * N_DIM, group, BLOCK), ("z",) + DIM)
    inner = call(
        inner_kernel,
        shape((LIST, LIST, USERS_DEV), F32),
        3,
        3 << 30,
        16 << 20,
        scratch=[
            pltpu.VMEM((SLOTS, 128), F32),
            pltpu.VMEM((LIST, LIST, USERS_DEV), F32),
        ],
    )(fetched, inverse, counts)
    times = times.reshape(8, USERS_DEV, BLOCK)
    return call(final_kernel, shape((USERS_DEV, BLOCK), F32), 10, 1 << 30, 4 << 20)(
        fetched, inverse, inner, counts, user_rows, times, *pred
    )


def solution(mesh):
    fine = Mesh(mesh.devices.reshape(4, 2, 4, 8), ("y", "core", "x", "z"))
    in_specs = (P(ROWS, DIM), P(ROWS, DIM), P(ROWS, None), P(ROWS), P())
    return jax.shard_map(
        body, mesh=fine, in_specs=in_specs, out_specs=P(ROWS, DIM), check_vma=False
    )
```

```python
import jax
import jax.numpy as jnp
from jax import lax
from jax.experimental import pallas as pl
from jax.experimental.pallas import tpu as pltpu
from jax.sharding import Mesh, PartitionSpec as P

F32 = jnp.float32
BF16 = jnp.bfloat16
I32 = jnp.int32
ROWS = ("x", "z")
DIM = ("y", "core")
BLOCK = 256
LIST = 32
USERS_DEV = 64
SLOTS = USERS_DEV * LIST
ITEM_DEV = 1024
N_ROWS = 32
N_DIM = 8
PER = SLOTS // N_ROWS
CHUNK = 256
CHUNKS = SLOTS // CHUNK
WEIGHT = 32.0 / 32768.0
VMEM = pl.BlockSpec(memory_space=pltpu.VMEM)
SMEM = pl.BlockSpec(memory_space=pltpu.SMEM)


def iota(shape, dim):
    return lax.broadcasted_iota(I32, shape, dim)


def dot(a, b, ca=1, cb=0):
    return lax.dot_general(a, b, (((ca,), (cb,)), ((), ())), preferred_element_type=F32)


def split(a):
    top = a.astype(BF16)
    rest = a - top.astype(F32)
    mid = rest.astype(BF16)
    low = (rest - mid.astype(F32)).astype(BF16)
    return top, mid, low


def dot_split(a, b, ca=1, cb=0):
    n = a[0].shape[1 - ca]
    top = dot(jnp.concatenate(a, axis=1 - ca), b[0], ca, cb)
    mid = dot(jnp.concatenate(a[:2], axis=1 - ca), b[1], ca, cb)
    low = dot(a[0], b[2], ca, cb)
    small = top[2 * n :] + low + mid[n:]
    return (small + (top[n : 2 * n] + mid[:n])) + top[:n]


def dot_pieces(a, b, ca=1, cb=0):
    n = a[0].shape[1 - ca]
    all_rows = dot(jnp.concatenate(a, axis=1 - ca), b, ca, cb)
    return (all_rows[2 * n :] + all_rows[n : 2 * n]) + all_rows[:n]


def one_hot(column, width):
    hit = iota((column.shape[0], width), 1) == column
    return jnp.where(hit, 1.0, 0.0).astype(BF16)


def call(kernel, out_shape, n_in, flops, nbytes, scratch=(), in_specs=None):
    multi = isinstance(out_shape, (tuple, list))
    return pl.pallas_call(
        kernel,
        out_shape=out_shape,
        in_specs=in_specs or [VMEM] * n_in,
        out_specs=[VMEM] * len(out_shape) if multi else VMEM,
        scratch_shapes=list(scratch),
        compiler_params=pltpu.CompilerParams(vmem_limit_bytes=20 << 20),
        cost_estimate=pl.CostEstimate(flops=flops, bytes_accessed=nbytes, transcendentals=0),
    )


def chunk_column(array, c):
    width = array.shape[0]
    step = CHUNK // width
    return jnp.concatenate(
        [array[:, c * step + i : c * step + i + 1] for i in range(step)], axis=0
    )


def index_kernel(ids_ref, table_ref, diag_ref, pos_ref, sent_ref):
    table = table_ref[...]
    table_hi = (table >> 8).astype(F32).astype(BF16)
    table_lo = (table & 255).astype(F32).astype(BF16)
    lane = iota((CHUNK, 128), 1)
    before = jnp.where(
        iota((CHUNK, CHUNK), 0) > iota((CHUNK, CHUNK), 1), 1.0, 0.0
    ).astype(BF16)
    totals = jnp.zeros((1, 128), F32)
    asked = jnp.zeros((128, 128), F32)
    places = jnp.zeros((CHUNK, 128), I32)
    ids_all = ids_ref[...]
    for c in range(CHUNKS):
        ids = chunk_column(ids_all, c)
        picked = one_hot(ids >> 7, 256)
        values = dot(picked, table_hi) * 256.0 + dot(picked, table_lo)
        row = jnp.sum(jnp.where(lane == (ids & 127), values, 0.0), axis=1, keepdims=True)
        row = row.astype(I32)
        member = jnp.where(lane == (row >> 10), 1.0, 0.0)
        ranks = dot(before, member.astype(BF16)) + totals
        rank = jnp.sum(member * ranks, axis=1, keepdims=True).astype(I32)
        totals = totals + jnp.sum(member, axis=0, keepdims=True)
        places = jnp.where(lane == c, (row >> 10) * PER + rank, places)
        ranked = one_hot(rank, 128)
        high = member * ((row >> 5) & 31).astype(F32)
        low = member * (row & 31).astype(F32)
        asked = asked + dot(high.astype(BF16), ranked, 0, 0) * 32.0
        asked = asked + dot(low.astype(BF16), ranked, 0, 0)
    pos_ref[...] = places
    sent_ref[...] = jnp.zeros(sent_ref.shape, F32)
    sent_ref[:, :, :BLOCK] = diag_ref[...]
    for k in range(N_ROWS):
        sent_ref[k, 0:1, BLOCK:] = asked[k : k + 1, :]


def pick_kernel(came_ref, table_ref, rows_ref, diag_ref):
    table = table_ref[...]
    diag = came_ref[0, :, :BLOCK]
    for r in range(1, N_ROWS):
        diag = diag + came_ref[r, :, :BLOCK]
    diag_ref[...] = jnp.broadcast_to(diag[None], diag_ref.shape)
    asked = jnp.concatenate([came_ref[r, 0:1, BLOCK:] for r in range(N_ROWS)], axis=0)
    asked = jnp.transpose(asked).astype(I32)
    asked = asked[:PER, :]
    for c in range(CHUNKS):
        column = chunk_column(asked, c)
        rows = dot(one_hot(column, ITEM_DEV), table).astype(BF16)
        rows_ref[c * CHUNK : (c + 1) * CHUNK, :] = rows


def place_kernel(pos_ref, came_ref, users_ref, fetched_ref, pred_ref):
    came = came_ref[...]
    users = users_ref[...]
    lane = iota((LIST, USERS_DEV), 1)
    pred = jnp.zeros((LIST, USERS_DEV), F32)
    size = 4 * CHUNK
    for n in range(SLOTS // size):
        chosen = [one_hot(pos_ref[:, c : c + 1], SLOTS) for c in range(4 * n, 4 * n + 4)]
        rows = dot(jnp.concatenate(chosen, axis=0), came).astype(BF16)
        fetched_ref[n * size : (n + 1) * size, :] = rows
        cross = dot(rows, users, 1, 1)
        for i in range(size // LIST):
            user = n * (size // LIST) + i
            pred = jnp.where(lane == user, cross[i * LIST : (i + 1) * LIST, :], pred)
    pred_ref[...] = pred


def product_kernel(block_ref, *refs):
    users_refs, tables = refs[:4], refs[4 : 4 + N_DIM]
    out_refs, held, sems = refs[4 + N_DIM : -2], refs[-2], refs[-1]
    quarter = BLOCK // 4
    copies = [pltpu.make_async_copy(tables[i], held.at[i], sems.at[i]) for i in range(N_DIM)]
    for copy in copies:
        copy.start()
    scores = jnp.zeros((BLOCK, ITEM_DEV), F32)
    for i in range(N_DIM):
        block = block_ref[i]
        users = [u[:, block].astype(F32).reshape(quarter, BLOCK) for u in users_refs]
        users = jnp.concatenate(users, axis=0).astype(BF16)
        copies[i].wait()
        scores = scores + dot(users, held[i], 1, 1)
    pieces = split(scores)
    for i in range(N_DIM):
        times = dot_pieces(pieces, held[i])
        for n, out_ref in enumerate(out_refs):
            part = times[n * quarter : (n + 1) * quarter]
            out_ref[:, block_ref[i]] = part.reshape(8, quarter // 8, BLOCK)


def sweep(start):
    size, group = 128, 4
    lane = iota((size, size), 1)
    sub = iota((size, size), 0)
    row_lane = iota((1, size), 1)

    def eight(n, a):
        for k0 in range(0, 8, group):
            cols = [jnp.broadcast_to(a[:, k : k + 1], (size, size)) for k in range(k0, k0 + group)]
            rows = [a[k : k + 1, :] for k in range(k0, k0 + group)]
            for j in range(group):
                k = k0 + j
                inv = 1.0 / cols[j][k : k + 1, :]
                scaled = rows[j] * inv
                for m in range(j + 1, group):
                    low = cols[m][k : k + 1, :] * inv
                    factor = cols[j][k0 + m : k0 + m + 1, :]
                    cols[m] = jnp.where(sub == k, low, cols[m] - cols[j] * low)
                    rows[m] = jnp.where(row_lane == k, factor * inv, rows[m] - factor * scaled)
                a = jnp.where(lane == k, cols[j] * inv, a - cols[j] * scaled)
                a = jnp.where(sub == k, jnp.where(row_lane == k, -inv, scaled), a)
        a = pltpu.roll(a, size - 8, 1)
        return jnp.concatenate([a[8:], a[:8]], axis=0)

    return -lax.fori_loop(0, size // 8, eight, start)


def inverse_kernel(diag_ref, out_ref):
    half = BLOCK // 2
    eye = jnp.where(iota((half, half), 0) == iota((half, half), 1), 1.0, 0.0)
    upper = split(WEIGHT * diag_ref[:half, half:])
    lead = sweep(WEIGHT * diag_ref[:half, :half] + eye)
    mixed = split(dot_split(split(lead), upper))
    rest = WEIGHT * diag_ref[half:, half:] + eye - dot_split(upper, mixed, 0, 0)
    rest = sweep(rest)
    cross = dot_split(mixed, split(rest))
    out_ref[:half, :half] = lead + dot_split(split(cross), mixed, 1, 1)
    out_ref[:half, half:] = -cross
    out_ref[half:, :half] = -jnp.transpose(cross)
    out_ref[half:, half:] = rest


def inner_kernel(fetched_ref, inverse_ref, counts_ref, out_ref, folded, work):
    i0, i1, i2 = split(inverse_ref[...])
    same = iota((CHUNK, CHUNK), 0) // LIST == iota((CHUNK, CHUNK), 1) // LIST

    def chunk(c):
        part = slice(c * CHUNK, (c + 1) * CHUNK)
        rows = fetched_ref[part, :]
        scaled = (dot(rows, i2) + dot(rows, i1)) + dot(rows, i0)
        cross = dot_pieces(split(scaled), rows, 1, 1)
        cross = jnp.where(same, cross, 0.0)
        both = cross[:, :128] + cross[:, 128:]
        both = both + pltpu.roll(both, 64, 1)
        folded[part, :] = both + pltpu.roll(both, 32, 1)

    for c in range(CHUNKS):
        chunk(c)
    slot = iota((LIST, USERS_DEV), 0)
    live = jnp.where(slot < counts_ref[...], 1.0, 0.0)
    for a in range(LIST):
        mine = jnp.transpose(folded[pl.ds(a, USERS_DEV, stride=LIST), :])[:LIST, :]
        work[a] = mine * (live * live[a : a + 1, :]) + jnp.where(slot == a, 1.0, 0.0)

    def step(k, carry):
        row = work[k]
        pivot = work[k, pl.ds(k, 1), :]
        inv = 1.0 / pivot
        scaled = row * inv
        here = slot == k
        for a in range(LIST):
            factor = row[a : a + 1, :]
            work[a] = jnp.where(here, factor * inv, work[a] - factor * scaled)
        work[k] = jnp.where(here, -inv, scaled)
        return carry

    lax.fori_loop(0, LIST, step, 0)
    out_ref[...] = -work[...]


def spread(values):
    flat = jnp.transpose(values)
    wide = jnp.concatenate([flat] * 4, axis=1)
    wide = jnp.concatenate([wide] * (SLOTS // 128), axis=1)
    own = iota((USERS_DEV, SLOTS), 1) // LIST == iota((USERS_DEV, SLOTS), 0)
    return jnp.where(own, wide, 0.0)


def weigh(values, fetched):
    return dot_pieces(split(spread(values)), fetched)


def final_kernel(
    fetched_ref, inverse_ref, inner_ref, counts_ref, users_ref, times_ref, *refs
):
    pred_refs, out_ref = refs[:-1], refs[-1]
    fetched = fetched_ref[...]
    inverse = split(inverse_ref[...])
    own = users_ref[...].astype(F32)
    slot = iota((LIST, USERS_DEV), 0)
    live = jnp.where(slot < counts_ref[...], 1.0, 0.0)
    pred = pred_refs[0][...]
    for ref in pred_refs[1:]:
        pred = pred + ref[...]
    residual = live * (pred - 1.0)
    times = times_ref[0]
    for i in range(1, 8):
        times = times + times_ref[i]
    gradient = weigh(residual, fetched) + WEIGHT * times + own
    scaled = dot_split(split(gradient), inverse)
    cross = dot(fetched, jnp.concatenate(split(scaled), axis=0), 1, 1)
    lane = lax.rem(iota((LIST, 3 * USERS_DEV), 1), USERS_DEV)
    found = jnp.zeros((LIST, 3 * USERS_DEV), F32)
    for user in range(USERS_DEV):
        found = jnp.where(lane == user, cross[user * LIST : (user + 1) * LIST, :], found)
    projected = found[:, 2 * USERS_DEV :] + found[:, USERS_DEV : 2 * USERS_DEV]
    projected = (projected + found[:, :USERS_DEV]) * live
    weights = jnp.zeros((LIST, USERS_DEV), F32)
    for a in range(LIST):
        weights = weights + inner_ref[a] * projected[a : a + 1, :]
    weights = weights * live
    back = dot_split(split(weigh(weights, fetched)), inverse)
    out_ref[...] = own - (scaled - back)


def shape(dims, dtype):
    return jax.ShapeDtypeStruct(dims, dtype)


def shift(x, axis, by):
    size = {"x": 4, "y": 4, "core": 2}[axis]
    return lax.ppermute(x, axis, [(i, (i + by) % size) for i in range(size)])


def gather_dims(table):
    tables = [table] + [shift(table, "y", 4 - i) for i in (1, 3)]
    far = shift(table, "y", 2)
    swapped = [shift(t, "core", 1) for t in tables]
    tables = tables + [far] + swapped + [shift(far, "core", 1)]
    y = lax.axis_index("y")
    core = lax.axis_index("core")
    blocks = [((y + i) % 4) * 2 + (core + j) % 2 for j in (0, 1) for i in (0, 1, 3, 2)]
    return tables, jnp.stack(blocks).astype(I32)


def exchange(x, axes):
    return lax.all_to_all(x, axes, 0, 0, tiled=True)


def body(user_rows, item_table, observed_items, counts, item_row):
    group = USERS_DEV // N_DIM
    slice_rows = BLOCK // N_ROWS
    users = user_rows.reshape(1, N_DIM, group, BLOCK)
    users = jnp.broadcast_to(users, (8, N_DIM, group, BLOCK))
    users = exchange(users.reshape(8 * N_DIM, group, BLOCK), ("z",) + DIM)
    tables, blocks = gather_dims(item_table)
    diag = dot(item_table, item_table, 0, 0).reshape(N_ROWS, slice_rows, BLOCK)
    pos, sent = call(
        index_kernel, (shape((CHUNK, 128), I32), shape((N_ROWS, 8, BLOCK + 128), F32)), 3, 1 << 30, 4 << 20
    )(observed_items.T, item_row.reshape(256, 128), diag)
    came = exchange(sent, ROWS)
    users = users.reshape(8, N_DIM, group, BLOCK)
    users = [users] + [shift(users, "x", 4 - i) for i in range(1, 4)]
    rows, diag = call(
        pick_kernel,
        (shape((SLOTS, BLOCK), BF16), shape((N_ROWS, slice_rows, BLOCK), F32)),
        2,
        1 << 30,
        4 << 20,
    )(came, item_table)
    came = exchange(rows.reshape(N_ROWS, PER, BLOCK), ROWS).reshape(SLOTS, BLOCK)
    diag = exchange(diag, ROWS)
    times = call(
        product_kernel,
        [shape((8, N_DIM, group, BLOCK), F32)] * 4,
        5 + len(tables),
        4 << 30,
        8 << 20,
        scratch=[
            pltpu.VMEM((N_DIM, ITEM_DEV, BLOCK), BF16),
            pltpu.SemaphoreType.DMA((N_DIM,)),
        ],
        in_specs=[SMEM] + [VMEM] * 4 + [pl.BlockSpec(memory_space=pl.ANY)] * N_DIM,
    )(blocks, *users, *tables)
    far = shift(times[2], "x", 2)
    times = [times[0], far] + [shift(times[i], "x", i) for i in (1, 3)]
    inverse = call(
        inverse_kernel, shape((BLOCK, BLOCK), F32), 1, 4 << 30, 8 << 20
    )(diag.reshape(BLOCK, BLOCK))
    counts = counts.reshape(1, USERS_DEV)
    fetched, pred = call(
        place_kernel,
        (shape((SLOTS, BLOCK), BF16), shape((LIST, USERS_DEV), F32)),
        3,
        3 << 30,
        8 << 20,
    )(pos, came, user_rows)
    pred = pred + shift(pred, "core", 1)
    pred = [pred] + [shift(pred, "y", i) for i in range(1, 4)]
    times = (times[0] + times[1]) + (times[2] + times[3])
    times = exchange(times.reshape(8 * N_DIM, group, BLOCK), ("z",) + DIM)
    inner = call(
        inner_kernel,
        shape((LIST, LIST, USERS_DEV), F32),
        3,
        3 << 30,
        16 << 20,
        scratch=[
            pltpu.VMEM((SLOTS, 128), F32),
            pltpu.VMEM((LIST, LIST, USERS_DEV), F32),
        ],
    )(fetched, inverse, counts)
    times = times.reshape(8, USERS_DEV, BLOCK)
    return call(final_kernel, shape((USERS_DEV, BLOCK), F32), 10, 1 << 30, 4 << 20)(
        fetched, inverse, inner, counts, user_rows, times, *pred
    )


def solution(mesh):
    fine = Mesh(mesh.devices.reshape(4, 2, 4, 8), ("y", "core", "x", "z"))
    in_specs = (P(ROWS, DIM), P(ROWS, DIM), P(ROWS, None), P(ROWS), P())
    return jax.shard_map(
        body, mesh=fine, in_specs=in_specs, out_specs=P(ROWS, DIM), check_vma=False
    )
```

```python
import jax
import jax.numpy as jnp
from jax import lax
from jax.experimental import pallas as pl
from jax.experimental.pallas import tpu as pltpu
from jax.sharding import Mesh, PartitionSpec as P

F32 = jnp.float32
BF16 = jnp.bfloat16
I32 = jnp.int32
ROWS = ("x", "z")
DIM = ("y", "core")
BLOCK = 256
LIST = 32
USERS_DEV = 64
SLOTS = USERS_DEV * LIST
ITEM_DEV = 1024
N_ROWS = 32
N_DIM = 8
PER = SLOTS // N_ROWS
CHUNK = 256
CHUNKS = SLOTS // CHUNK
WEIGHT = 32.0 / 32768.0
VMEM = pl.BlockSpec(memory_space=pltpu.VMEM)
SMEM = pl.BlockSpec(memory_space=pltpu.SMEM)


def iota(shape, dim):
    return lax.broadcasted_iota(I32, shape, dim)


def dot(a, b, ca=1, cb=0):
    return lax.dot_general(a, b, (((ca,), (cb,)), ((), ())), preferred_element_type=F32)


def split(a):
    top = a.astype(BF16)
    rest = a - top.astype(F32)
    mid = rest.astype(BF16)
    low = (rest - mid.astype(F32)).astype(BF16)
    return top, mid, low


def dot_split(a, b, ca=1, cb=0):
    n = a[0].shape[1 - ca]
    top = dot(jnp.concatenate(a, axis=1 - ca), b[0], ca, cb)
    mid = dot(jnp.concatenate(a[:2], axis=1 - ca), b[1], ca, cb)
    low = dot(a[0], b[2], ca, cb)
    small = top[2 * n :] + low + mid[n:]
    return (small + (top[n : 2 * n] + mid[:n])) + top[:n]


def dot_pieces(a, b, ca=1, cb=0):
    n = a[0].shape[1 - ca]
    all_rows = dot(jnp.concatenate(a, axis=1 - ca), b, ca, cb)
    return (all_rows[2 * n :] + all_rows[n : 2 * n]) + all_rows[:n]


def one_hot(column, width):
    hit = iota((column.shape[0], width), 1) == column
    return jnp.where(hit, 1.0, 0.0).astype(BF16)


def call(kernel, out_shape, n_in, flops, nbytes, scratch=(), in_specs=None):
    multi = isinstance(out_shape, (tuple, list))
    return pl.pallas_call(
        kernel,
        out_shape=out_shape,
        in_specs=in_specs or [VMEM] * n_in,
        out_specs=[VMEM] * len(out_shape) if multi else VMEM,
        scratch_shapes=list(scratch),
        compiler_params=pltpu.CompilerParams(vmem_limit_bytes=20 << 20),
        cost_estimate=pl.CostEstimate(flops=flops, bytes_accessed=nbytes, transcendentals=0),
    )


def chunk_column(array, c):
    width = array.shape[0]
    step = CHUNK // width
    return jnp.concatenate(
        [array[:, c * step + i : c * step + i + 1] for i in range(step)], axis=0
    )


def index_kernel(ids_ref, table_ref, diag_ref, pos_ref, sent_ref):
    table = table_ref[...]
    table_hi = (table >> 8).astype(F32).astype(BF16)
    table_lo = (table & 255).astype(F32).astype(BF16)
    lane = iota((CHUNK, 128), 1)
    before = jnp.where(
        iota((CHUNK, CHUNK), 0) > iota((CHUNK, CHUNK), 1), 1.0, 0.0
    ).astype(BF16)
    totals = jnp.zeros((1, 128), F32)
    asked = jnp.zeros((128, 128), F32)
    places = jnp.zeros((CHUNK, 128), I32)
    ids_all = ids_ref[...]
    for c in range(CHUNKS):
        ids = chunk_column(ids_all, c)
        picked = one_hot(ids >> 7, 256)
        values = dot(picked, table_hi) * 256.0 + dot(picked, table_lo)
        row = jnp.sum(jnp.where(lane == (ids & 127), values, 0.0), axis=1, keepdims=True)
        row = row.astype(I32)
        member = jnp.where(lane == (row >> 10), 1.0, 0.0)
        ranks = dot(before, member.astype(BF16)) + totals
        rank = jnp.sum(member * ranks, axis=1, keepdims=True).astype(I32)
        totals = totals + jnp.sum(member, axis=0, keepdims=True)
        places = jnp.where(lane == c, (row >> 10) * PER + rank, places)
        ranked = one_hot(rank, 128)
        high = member * ((row >> 5) & 31).astype(F32)
        low = member * (row & 31).astype(F32)
        asked = asked + dot(high.astype(BF16), ranked, 0, 0) * 32.0
        asked = asked + dot(low.astype(BF16), ranked, 0, 0)
    pos_ref[...] = places
    sent_ref[...] = jnp.zeros(sent_ref.shape, F32)
    sent_ref[:, :, :BLOCK] = diag_ref[...]
    for k in range(N_ROWS):
        sent_ref[k, 0:1, BLOCK:] = asked[k : k + 1, :]


def pick_kernel(came_ref, table_ref, rows_ref, diag_ref):
    table = table_ref[...]
    diag = came_ref[0, :, :BLOCK]
    for r in range(1, N_ROWS):
        diag = diag + came_ref[r, :, :BLOCK]
    diag_ref[...] = jnp.broadcast_to(diag[None], diag_ref.shape)
    asked = jnp.concatenate([came_ref[r, 0:1, BLOCK:] for r in range(N_ROWS)], axis=0)
    asked = jnp.transpose(asked).astype(I32)
    asked = asked[:PER, :]
    for c in range(CHUNKS):
        column = chunk_column(asked, c)
        rows = dot(one_hot(column, ITEM_DEV), table).astype(BF16)
        rows_ref[c * CHUNK : (c + 1) * CHUNK, :] = rows


def place_kernel(pos_ref, came_ref, users_ref, fetched_ref, pred_ref):
    came = came_ref[...]
    users = users_ref[...]
    lane = iota((LIST, USERS_DEV), 1)
    pred = jnp.zeros((LIST, USERS_DEV), F32)
    size = 4 * CHUNK
    for n in range(SLOTS // size):
        chosen = [one_hot(pos_ref[:, c : c + 1], SLOTS) for c in range(4 * n, 4 * n + 4)]
        rows = dot(jnp.concatenate(chosen, axis=0), came).astype(BF16)
        fetched_ref[n * size : (n + 1) * size, :] = rows
        cross = dot(rows, users, 1, 1)
        for i in range(size // LIST):
            user = n * (size // LIST) + i
            pred = jnp.where(lane == user, cross[i * LIST : (i + 1) * LIST, :], pred)
    pred_ref[...] = pred


def product_kernel(block_ref, *refs):
    users_refs, tables = refs[:4], refs[4 : 4 + N_DIM]
    out_refs, held, sems = refs[4 + N_DIM : -2], refs[-2], refs[-1]
    quarter = BLOCK // 4
    copies = [pltpu.make_async_copy(tables[i], held.at[i], sems.at[i]) for i in range(N_DIM)]
    for copy in copies:
        copy.start()
    scores = jnp.zeros((BLOCK, ITEM_DEV), F32)
    for i in range(N_DIM):
        block = block_ref[i]
        users = [u[:, block].astype(F32).reshape(quarter, BLOCK) for u in users_refs]
        users = jnp.concatenate(users, axis=0).astype(BF16)
        copies[i].wait()
        scores = scores + dot(users, held[i], 1, 1)
    pieces = split(scores)
    for i in range(N_DIM):
        times = dot_pieces(pieces, held[i])
        for n, out_ref in enumerate(out_refs):
            part = times[n * quarter : (n + 1) * quarter]
            out_ref[:, block_ref[i]] = part.reshape(8, quarter // 8, BLOCK)


def sweep(start):
    size, group = 128, 4
    lane = iota((size, size), 1)
    sub = iota((size, size), 0)
    row_lane = iota((1, size), 1)

    def eight(n, a):
        for k0 in range(0, 8, group):
            cols = [jnp.broadcast_to(a[:, k : k + 1], (size, size)) for k in range(k0, k0 + group)]
            rows = [a[k : k + 1, :] for k in range(k0, k0 + group)]
            for j in range(group):
                k = k0 + j
                inv = 1.0 / cols[j][k : k + 1, :]
                scaled = rows[j] * inv
                for m in range(j + 1, group):
                    low = cols[m][k : k + 1, :] * inv
                    factor = cols[j][k0 + m : k0 + m + 1, :]
                    cols[m] = jnp.where(sub == k, low, cols[m] - cols[j] * low)
                    rows[m] = jnp.where(row_lane == k, factor * inv, rows[m] - factor * scaled)
                a = jnp.where(lane == k, cols[j] * inv, a - cols[j] * scaled)
                a = jnp.where(sub == k, jnp.where(row_lane == k, -inv, scaled), a)
        a = pltpu.roll(a, size - 8, 1)
        return jnp.concatenate([a[8:], a[:8]], axis=0)

    return -lax.fori_loop(0, size // 8, eight, start)


def inverse_kernel(diag_ref, out_ref):
    half = BLOCK // 2
    eye = jnp.where(iota((half, half), 0) == iota((half, half), 1), 1.0, 0.0)
    upper = split(WEIGHT * diag_ref[:half, half:])
    lead = sweep(WEIGHT * diag_ref[:half, :half] + eye)
    mixed = split(dot_split(split(lead), upper))
    rest = WEIGHT * diag_ref[half:, half:] + eye - dot_split(upper, mixed, 0, 0)
    rest = sweep(rest)
    cross = dot_split(mixed, split(rest))
    out_ref[:half, :half] = lead + dot_split(split(cross), mixed, 1, 1)
    out_ref[:half, half:] = -cross
    out_ref[half:, :half] = -jnp.transpose(cross)
    out_ref[half:, half:] = rest


def inner_kernel(fetched_ref, inverse_ref, counts_ref, out_ref, folded, work):
    i0, i1, i2 = split(inverse_ref[...])
    same = iota((CHUNK, CHUNK), 0) // LIST == iota((CHUNK, CHUNK), 1) // LIST

    def chunk(c):
        part = slice(c * CHUNK, (c + 1) * CHUNK)
        rows = fetched_ref[part, :]
        scaled = (dot(rows, i2) + dot(rows, i1)) + dot(rows, i0)
        cross = dot_pieces(split(scaled), rows, 1, 1)
        cross = jnp.where(same, cross, 0.0)
        both = cross[:, :128] + cross[:, 128:]
        both = both + pltpu.roll(both, 64, 1)
        folded[part, :] = both + pltpu.roll(both, 32, 1)

    for c in range(CHUNKS):
        chunk(c)
    slot = iota((LIST, USERS_DEV), 0)
    live = jnp.where(slot < counts_ref[...], 1.0, 0.0)
    for a in range(LIST):
        mine = jnp.transpose(folded[pl.ds(a, USERS_DEV, stride=LIST), :])[:LIST, :]
        work[a] = mine * (live * live[a : a + 1, :]) + jnp.where(slot == a, 1.0, 0.0)

    def step(k, carry):
        row = work[k]
        pivot = work[k, pl.ds(k, 1), :]
        inv = 1.0 / pivot
        scaled = row * inv
        here = slot == k
        for a in range(LIST):
            factor = row[a : a + 1, :]
            work[a] = jnp.where(here, factor * inv, work[a] - factor * scaled)
        work[k] = jnp.where(here, -inv, scaled)
        return carry

    lax.fori_loop(0, LIST, step, 0)
    out_ref[...] = -work[...]


def spread(values):
    flat = jnp.transpose(values)
    wide = jnp.concatenate([flat] * 4, axis=1)
    wide = jnp.concatenate([wide] * (SLOTS // 128), axis=1)
    own = iota((USERS_DEV, SLOTS), 1) // LIST == iota((USERS_DEV, SLOTS), 0)
    return jnp.where(own, wide, 0.0)


def weigh(values, fetched):
    return dot_pieces(split(spread(values)), fetched)


def final_kernel(
    fetched_ref, inverse_ref, inner_ref, counts_ref, users_ref, times_ref, *refs
):
    pred_refs, out_ref = refs[:-1], refs[-1]
    fetched = fetched_ref[...]
    inverse = split(inverse_ref[...])
    own = users_ref[...].astype(F32)
    slot = iota((LIST, USERS_DEV), 0)
    live = jnp.where(slot < counts_ref[...], 1.0, 0.0)
    pred = pred_refs[0][...]
    for ref in pred_refs[1:]:
        pred = pred + ref[...]
    residual = live * (pred - 1.0)
    times = times_ref[0]
    for i in range(1, 8):
        times = times + times_ref[i]
    gradient = weigh(residual, fetched) + WEIGHT * times + own
    scaled = dot_split(split(gradient), inverse)
    cross = dot(fetched, jnp.concatenate(split(scaled), axis=0), 1, 1)
    lane = lax.rem(iota((LIST, 3 * USERS_DEV), 1), USERS_DEV)
    found = jnp.zeros((LIST, 3 * USERS_DEV), F32)
    for user in range(USERS_DEV):
        found = jnp.where(lane == user, cross[user * LIST : (user + 1) * LIST, :], found)
    projected = found[:, 2 * USERS_DEV :] + found[:, USERS_DEV : 2 * USERS_DEV]
    projected = (projected + found[:, :USERS_DEV]) * live
    weights = jnp.zeros((LIST, USERS_DEV), F32)
    for a in range(LIST):
        weights = weights + inner_ref[a] * projected[a : a + 1, :]
    weights = weights * live
    back = dot_split(split(weigh(weights, fetched)), inverse)
    out_ref[...] = own - (scaled - back)


def shape(dims, dtype):
    return jax.ShapeDtypeStruct(dims, dtype)


def shift(x, axis, by):
    size = {"x": 4, "y": 4, "core": 2}[axis]
    return lax.ppermute(x, axis, [(i, (i + by) % size) for i in range(size)])


def gather_dims(table):
    tables = [table] + [shift(table, "y", 4 - i) for i in (1, 3)]
    far = shift(table, "y", 2)
    swapped = [shift(t, "core", 1) for t in tables]
    tables = tables + [far] + swapped + [shift(far, "core", 1)]
    y = lax.axis_index("y")
    core = lax.axis_index("core")
    blocks = [((y + i) % 4) * 2 + (core + j) % 2 for j in (0, 1) for i in (0, 1, 3, 2)]
    return tables, jnp.stack(blocks).astype(I32)


def exchange(x, axes):
    return lax.all_to_all(x, axes, 0, 0, tiled=True)


def body(user_rows, item_table, observed_items, counts, item_row):
    group = USERS_DEV // N_DIM
    slice_rows = BLOCK // N_ROWS
    users = user_rows.reshape(1, N_DIM, group, BLOCK)
    users = jnp.broadcast_to(users, (8, N_DIM, group, BLOCK))
    users = exchange(users.reshape(8 * N_DIM, group, BLOCK), ("z",) + DIM)
    tables, blocks = gather_dims(item_table)
    diag = dot(item_table, item_table, 0, 0).reshape(N_ROWS, slice_rows, BLOCK)
    pos, sent = call(
        index_kernel, (shape((CHUNK, 128), I32), shape((N_ROWS, 8, BLOCK + 128), F32)), 3, 1 << 30, 4 << 20
    )(observed_items.T, item_row.reshape(256, 128), diag)
    came = exchange(sent, ROWS)
    users = users.reshape(8, N_DIM, group, BLOCK)
    users = [users] + [shift(users, "x", 4 - i) for i in range(1, 4)]
    rows, diag = call(
        pick_kernel,
        (shape((SLOTS, BLOCK), BF16), shape((N_ROWS, slice_rows, BLOCK), F32)),
        2,
        1 << 30,
        4 << 20,
    )(came, item_table)
    came = exchange(rows.reshape(N_ROWS, PER, BLOCK), ROWS).reshape(SLOTS, BLOCK)
    diag = exchange(diag, ROWS)
    times = call(
        product_kernel,
        [shape((8, N_DIM, group, BLOCK), F32)] * 4,
        5 + len(tables),
        4 << 30,
        8 << 20,
        scratch=[
            pltpu.VMEM((N_DIM, ITEM_DEV, BLOCK), BF16),
            pltpu.SemaphoreType.DMA((N_DIM,)),
        ],
        in_specs=[SMEM] + [VMEM] * 4 + [pl.BlockSpec(memory_space=pl.ANY)] * N_DIM,
    )(blocks, *users, *tables)
    far = shift(times[2], "x", 2)
    one = shift(times[1], "x", 1)
    times = [times[0], far, shift(times[3], "x", 3)]
    inverse = call(
        inverse_kernel, shape((BLOCK, BLOCK), F32), 1, 4 << 30, 8 << 20
    )(diag.reshape(BLOCK, BLOCK))
    counts = counts.reshape(1, USERS_DEV)
    fetched, pred = call(
        place_kernel,
        (shape((SLOTS, BLOCK), BF16), shape((LIST, USERS_DEV), F32)),
        3,
        3 << 30,
        8 << 20,
    )(pos, came, user_rows)
    pred = pred + shift(pred, "core", 1)
    pred = [pred] + [shift(pred, "y", i) for i in range(1, 4)]
    early = (times[0] + times[1]) + times[2]
    times = lax.optimization_barrier(early) + one
    times = exchange(times.reshape(8 * N_DIM, group, BLOCK), ("z",) + DIM)
    inner = call(
        inner_kernel,
        shape((LIST, LIST, USERS_DEV), F32),
        3,
        3 << 30,
        16 << 20,
        scratch=[
            pltpu.VMEM((SLOTS, 128), F32),
            pltpu.VMEM((LIST, LIST, USERS_DEV), F32),
        ],
    )(fetched, inverse, counts)
    times = times.reshape(8, USERS_DEV, BLOCK)
    return call(final_kernel, shape((USERS_DEV, BLOCK), F32), 10, 1 << 30, 4 << 20)(
        fetched, inverse, inner, counts, user_rows, times, *pred
    )


def solution(mesh):
    fine = Mesh(mesh.devices.reshape(4, 2, 4, 8), ("y", "core", "x", "z"))
    in_specs = (P(ROWS, DIM), P(ROWS, DIM), P(ROWS, None), P(ROWS), P())
    return jax.shard_map(
        body, mesh=fine, in_specs=in_specs, out_specs=P(ROWS, DIM), check_vma=False
    )
```
